128 devices in a mesh: layer: 16 (over x_lo, y, core), dp: 8 (over x_hi, z).
Axes of the slice: x: 4 (x_hi: 2, x_lo: 2; x = x_hi * 2 + x_lo), y: 4, z: 4, core: 2. Of those that a mesh axis runs over, the one named last changes fastest.
Arguments:
- activations: bfloat16 [16, 2048, 2048], P('layer', 'dp')
- factor_old: float32 [16, 2048, 2048], P('layer', 'dp'), as said below
- cross_old: float32 [16, 2048, 2048], P('layer', 'dp')
- gradients: bfloat16 [16, 2048, 1024], P('layer', 'dp'), may hold values from -6 to 6
- moments: bfloat16 [16, 2048, 1024], P('layer', 'dp'), may hold values from -6 to 6
- exponents: int32 [16, 16], P('layer', 'dp'), may hold values from -3 to 2
- master: float32 [16, 2048, 1024], P('layer', 'dp'), may hold values from -6 to 6
Outputs:
- factor_new: float32 [16, 2048, 2048], P('layer', 'dp')
- cross_new: float32 [16, 2048, 2048], P('layer', 'dp')
- moments_new: bfloat16 [16, 2048, 1024], P('layer', 'dp')
- master_new: float32 [16, 2048, 1024], P('layer', 'dp')
- replicas: bfloat16 [16, 2048, 1024], P('layer')
The draws below stay inside these ranges and needn't reach their ends.
Inputs may be any that keep to these rules, and one draw needn't show every extreme that they name: factor_old is symmetric in its last two dimensions, and its diagonal entries lie between 0.6 and 1.4.
All inputs are finite; a program needn't handle non-finite values.
Results may differ from the reference program's by a relative error of at most 0.0025.
Values may be sent and summed in bfloat16 or wider, within the bound.
No kernel may reach another device: no remote copies, remote signals or barrier semaphores. Data moves between devices by JAX's collectives and lax.ppermute only.
A program may use at most 128 MiB of HBM per device.

```python
import jax
import jax.numpy as jnp
from jax import lax

FEATURES = 2048
OUTPUTS = 1024
SCALE_BLOCK = 128
LAYERS = 16
TOKENS = 2048


def draw_activations(key, part):
    subkeys = jax.random.split(jax.random.fold_in(key, 101), 2)
    persist = jax.random.uniform(subkeys[0], (FEATURES,), jnp.float32, 0.3, 0.95)
    noise = jax.random.normal(subkeys[1], (LAYERS, TOKENS, FEATURES), jnp.float32)
    renewal = jnp.sqrt(1.0 - persist * persist)

    def advance(previous, layer_noise):
        following = persist * previous + renewal * layer_noise
        return (following, following)
    _, stacked = lax.scan(advance, noise[0], noise[1:])
    result = jnp.concatenate([noise[0][None], stacked], 0)
    return result.astype(jnp.bfloat16)


def draw_factor_old(key, part):
    subkeys = jax.random.split(jax.random.fold_in(key, 202), 2)
    diagonal_values = jax.random.uniform(subkeys[0], (LAYERS, FEATURES), jnp.float32, 0.6, 1.4)
    raw = jax.random.normal(subkeys[1], (LAYERS, FEATURES, FEATURES), jnp.float32)
    raw = raw * (0.3 / jnp.sqrt(jnp.float32(FEATURES)))
    symmetric = (raw + jnp.swapaxes(raw, 1, 2)) * 0.70710678
    identity = jnp.eye(FEATURES, dtype=jnp.float32)
    return symmetric * (1.0 - identity) + diagonal_values[:, :, None] * identity


def draw_cross_old(key, part):
    subkeys = jax.random.split(jax.random.fold_in(key, 303), 2)
    diagonal_values = jax.random.uniform(subkeys[0], (LAYERS, FEATURES), jnp.float32, 0.2, 0.9)
    raw = jax.random.normal(subkeys[1], (LAYERS, FEATURES, FEATURES), jnp.float32)
    raw = raw * (0.3 / jnp.sqrt(jnp.float32(FEATURES)))
    identity = jnp.eye(FEATURES, dtype=jnp.float32)
    return raw * (1.0 - identity) + diagonal_values[:, :, None] * identity


def touch_ends(drawn, own_key, least, largest):
    spot = [jax.random.randint(jax.random.fold_in(own_key, axis), (), 0, length) for axis, length in enumerate(drawn.shape)]
    longest = drawn.shape.index(max(drawn.shape))
    beside = spot[:longest] + [(spot[longest] + 1) % drawn.shape[longest]] + spot[longest + 1:]
    return drawn.at[tuple(spot)].set(least).at[tuple(beside)].set(largest)


def block_levels(key, extent, cuts, low, largest):
    def one(dim, blocks):
        draws = jax.random.uniform(jax.random.fold_in(jax.random.fold_in(key, 6), dim), (blocks,), jnp.float32, low / len(cuts), largest / len(cuts))
        return jnp.repeat(jnp.exp(draws), extent[dim] // blocks).reshape((-1,) + (1,) * (len(extent) - dim - 1))

    gain = one(*cuts[0])
    for cut in cuts[1:]:
        gain = gain * one(*cut)
    return gain


def centred(stream_key, extent, deviation, most, shards=(), kind=jnp.bfloat16):
    values = deviation * jax.random.normal(stream_key, extent, jnp.float32)
    if shards:
        values = values * block_levels(stream_key, extent, shards, -0.22, 0.18)
    return jnp.clip(values, -most, most).astype(kind)


def setup_inputs(seed: int = 0) -> dict:
    arg_keys = jax.random.split(jax.random.key(seed), 8)
    activations = draw_activations(jax.random.fold_in(arg_keys[7], 71), 0)
    factor_old = draw_factor_old(jax.random.fold_in(arg_keys[7], 71), 0)
    cross_old = draw_cross_old(jax.random.fold_in(arg_keys[7], 71), 0)
    gradients = centred(arg_keys[3], (LAYERS, FEATURES, OUTPUTS), 1.0, 6.0, ((0, 16), (1, 8)))
    moments = centred(arg_keys[4], (LAYERS, FEATURES, OUTPUTS), 1.0, 6.0, ((0, 16), (1, 8)))
    exponents = touch_ends(jax.random.randint(arg_keys[5], (LAYERS, FEATURES // SCALE_BLOCK), -3, 3), jax.random.fold_in(arg_keys[5], 1), -3, 2).astype(jnp.int32)
    master = centred(arg_keys[6], (LAYERS, FEATURES, OUTPUTS), 1.0, 6.0, ((0, 16), (1, 8)), jnp.float32)
    return dict(activations=activations, factor_old=factor_old, cross_old=cross_old, gradients=gradients, moments=moments, exponents=exponents, master=master)


FACTOR_DECAY = 0.9
DAMPING = 0.5
MOMENTUM = 0.8
STEP_SIZE = 0.05


def chain_solve(target, pivots, coupling):
    coupling_ratio = coupling / pivots

    def forward_step(passed, slices):
        target_layer, pivot_layer, coupled = slices
        scaled = (target_layer - passed) / pivot_layer[:, None]
        return coupled[:, None] * scaled, scaled

    zero_block = jnp.zeros(target.shape[1:], jnp.float32)
    _, scaled_all = lax.scan(forward_step, zero_block, (target, pivots, coupling))

    def backward_step(nearer, slices):
        scaled, ratio_layer = slices
        solved = scaled - ratio_layer[:, None] * nearer
        return solved, solved

    _, solved_all = lax.scan(backward_step, zero_block, (scaled_all, coupling_ratio), reverse=True)
    return solved_all


def reference(activations, factor_old, cross_old, gradients, moments, exponents, master):
    fresh_weight = (1.0 - FACTOR_DECAY) / TOKENS
    next_acts = jnp.concatenate([activations[1:], jnp.zeros_like(activations[:1])], 0)

    def refresh(slices):
        own_layer, next_layer, factor_prev, cross_prev = slices
        batch_factor = jnp.dot(own_layer.T, own_layer, preferred_element_type=jnp.float32)
        batch_cross = jnp.dot(own_layer.T, next_layer, preferred_element_type=jnp.float32)
        return (FACTOR_DECAY * factor_prev + fresh_weight * batch_factor,
                FACTOR_DECAY * cross_prev + fresh_weight * batch_cross)

    factor_new, cross_new = lax.map(refresh, (activations, next_acts, factor_old, cross_old))
    diag_index = jnp.arange(FEATURES)
    pivots = DAMPING + factor_new[:, diag_index, diag_index]
    coupling = cross_new[:, diag_index, diag_index]
    grad_wide = gradients.astype(jnp.float32)
    initial = chain_solve(grad_wide, pivots, coupling).astype(jnp.bfloat16)
    initial_wide = initial.astype(jnp.float32)
    zero_sol = jnp.zeros_like(initial_wide[:1])
    upper_sol = jnp.concatenate([initial_wide[1:], zero_sol], 0)
    lower_sol = jnp.concatenate([zero_sol, initial_wide[:-1]], 0)
    cross_lower = jnp.concatenate([jnp.zeros_like(cross_new[:1]), cross_new[:-1]], 0)

    def apply_blocks(slices):
        factor_layer, cross_layer, cross_prev, own_block, upper_block, lower_block = slices
        result = jnp.dot(factor_layer, own_block, precision=lax.Precision.HIGHEST, preferred_element_type=jnp.float32)
        result = result + DAMPING * own_block
        result = result + jnp.dot(cross_layer, upper_block, precision=lax.Precision.HIGHEST, preferred_element_type=jnp.float32)
        result = result + jnp.dot(cross_prev.T, lower_block, precision=lax.Precision.HIGHEST, preferred_element_type=jnp.float32)
        return result

    applied = lax.map(apply_blocks, (factor_new, cross_new, cross_lower, initial_wide, upper_sol, lower_sol))
    update = initial_wide + chain_solve(grad_wide - applied, pivots, coupling)
    dequant = jnp.repeat(jnp.exp2(exponents.astype(jnp.float32)), SCALE_BLOCK, axis=1)[:, :, None]
    requant = jnp.repeat(jnp.exp2(-exponents.astype(jnp.float32)), SCALE_BLOCK, axis=1)[:, :, None]
    moment = MOMENTUM * moments.astype(jnp.float32) * dequant + (1.0 - MOMENTUM) * update
    moments_new = (moment * requant).astype(jnp.bfloat16)
    master_new = master - STEP_SIZE * moment
    replicas = master_new.astype(jnp.bfloat16)
    return factor_new, cross_new, moments_new, master_new, replicas
```

```python
import jax
import jax.numpy as jnp
from jax import lax
from jax.experimental import pallas as pl
from jax.experimental.pallas import tpu as pltpu
from jax.sharding import Mesh
from jax.sharding import PartitionSpec as P

SCALE_BLOCK = 128
LAYER = ("layer_0", "layer_1", "layer_2")
DP = ("dp_0", "dp_1")
LAYERS = 16
GROUP = 8
TURN = 4

FACTOR_DECAY = 0.9
DAMPING = 0.5
MOMENTUM = 0.8
STEP_SIZE = 0.05

F32 = jnp.float32
BF16 = jnp.bfloat16


def along_layers(value, steps):
    pairs = [(i, i + steps) for i in range(LAYERS) if 0 <= i + steps < LAYERS]
    return lax.ppermute(value, LAYER, pairs)


def turned(value, steps):
    return lax.ppermute(value, "dp_1", [(i, (i + steps) % TURN) for i in range(TURN)])


def across(value):
    return lax.ppermute(value, "dp_0", [(0, 1), (1, 0)])


def gathered(own):
    half = own.shape[0] // 2
    other = across(own)
    before = turned(own, 1)
    after = turned(own, 3)
    far = turned(after, 3)
    other_before = turned(other, 1)
    other_after = across(after)
    other_far = jnp.concatenate([turned(other_before[:half], 1), turned(other_after[half:], 3)], 0)
    return (own, before, far, after, other, other_before, other_far, other_after)


def piece_order():
    mine, turn = lax.axis_index("dp_0"), lax.axis_index("dp_1")
    side = jnp.stack([mine] * TURN + [1 - mine] * TURN)
    steps = jnp.array([0, 3, 2, 1, 0, 3, 2, 1], jnp.int32)
    return (side * TURN + (turn + steps) % TURN).astype(jnp.int32)


def halves(value):
    high = value.astype(BF16)
    return high, (value - high.astype(F32)).astype(BF16)


def transposed_dot(left, right):
    return lax.dot_general(left, right, (((0,), (0,)), ((), ())), preferred_element_type=F32)


def refresh_kernel(weight, order, *refs):
    pieces, (own, lower, upper, factor_old, row_old, col_old) = refs[:GROUP], refs[GROUP : GROUP + 6]
    factor, factor_hi, factor_lo, row_hi, row_lo, row_batch, col_hi, col_lo = refs[GROUP + 6 :]
    sums = [None, None, None]
    for k in range(GROUP):
        right = pieces[k][...]
        for n, left in enumerate((own, lower, upper)):
            part = transposed_dot(left[order[k]], right)
            sums[n] = part if k == 0 else sums[n] + part
    fresh = FACTOR_DECAY * factor_old[...] + weight * sums[0]
    factor[...] = fresh
    factor_hi[...], factor_lo[...] = halves(fresh)
    row_batch[...] = sums[1].astype(BF16)
    row_hi[...], row_lo[...] = halves(FACTOR_DECAY * row_old[...].astype(F32) + weight * sums[1])
    old = jnp.concatenate([col_old[b].astype(F32).T for b in range(col_old.shape[0])], 1)
    col_hi[...], col_lo[...] = halves(FACTOR_DECAY * old + weight * sums[2])


def refresh(weight, order, pieces, own, lower, upper, factor_old, row_old, col_old):
    rows, features = factor_old.shape
    tile = 512
    blocks = tile // rows
    column = pl.BlockSpec((rows, tile), lambda j, o: (0, j))
    whole = pl.BlockSpec((GROUP, rows, rows), lambda j, o: (0, 0, 0))
    stacked = pl.BlockSpec((blocks, rows, rows), lambda j, o: (j, 0, 0))
    shape = (rows, features)
    kinds = (F32, BF16, BF16, BF16, BF16, BF16, BF16, BF16)
    return pl.pallas_call(
        lambda *refs: refresh_kernel(weight, *refs),
        grid_spec=pltpu.PrefetchScalarGridSpec(
            num_scalar_prefetch=1,
            grid=(features // tile,),
            in_specs=[column] * GROUP + [whole] * 3 + [column, column, stacked],
            out_specs=[column] * len(kinds),
        ),
        out_shape=[jax.ShapeDtypeStruct(shape, kind) for kind in kinds],
        compiler_params=pltpu.CompilerParams(vmem_limit_bytes=48 * 2**20),
        name="refresh",
    )(order, *pieces, own, lower, upper, factor_old, row_old, col_old)


def apply_kernel(order, *refs):
    pieces, (factor_hi, factor_lo, row_hi, row_lo, col_hi, col_lo, grad) = refs[:GROUP], refs[GROUP : GROUP + 7]
    rest, down, up, joined = refs[GROUP + 7 :]
    rows = grad.shape[0]
    for k in range(GROUP):
        joined[pl.ds(pl.multiple_of(order[k] * rows, rows), rows), :] = pieces[k][...]
    full = joined[...]

    def product(high, low):
        return jnp.dot(high[...], full, preferred_element_type=F32) + jnp.dot(
            low[...], full, preferred_element_type=F32
        )

    applied = product(factor_hi, factor_lo) + DAMPING * pieces[0][...].astype(F32)
    rest[...] = grad[...].astype(F32) - applied
    down[...] = product(row_hi, row_lo).astype(down.dtype)
    up[...] = product(col_hi, col_lo).astype(up.dtype)


def apply_blocks(order, pieces, matrices, grad):
    rows, outputs = grad.shape
    features = matrices[0].shape[1]
    tile = 512
    column = pl.BlockSpec((rows, tile), lambda j, o: (0, j))
    whole = pl.BlockSpec((rows, features), lambda j, o: (0, 0))
    shape = (rows, outputs)
    return pl.pallas_call(
        apply_kernel,
        grid_spec=pltpu.PrefetchScalarGridSpec(
            num_scalar_prefetch=1,
            grid=(outputs // tile,),
            in_specs=[column] * GROUP + [whole] * 6 + [column],
            out_specs=[column] * 3,
            scratch_shapes=[pltpu.VMEM((features, tile), BF16)],
        ),
        out_shape=[jax.ShapeDtypeStruct(shape, kind) for kind in (F32, BF16, BF16)],
        compiler_params=pltpu.CompilerParams(vmem_limit_bytes=48 * 2**20),
        name="apply_blocks",
    )(order, *pieces, *matrices, grad)


def solve_kernel(target, inverse, coupling, ratio, solved):
    outputs = target.shape[-1]
    for start in range(0, outputs, 128):
        lanes = pl.ds(start, 128)
        passed = jnp.zeros(target.shape[1:2] + (128,), F32)
        scaled = []
        for layer in range(LAYERS):
            scaled.append((target[layer, :, lanes].astype(F32) - passed) * inverse[layer])
            passed = coupling[layer] * scaled[layer]
        nearer = jnp.zeros_like(passed)
        for layer in reversed(range(LAYERS)):
            nearer = scaled[layer] - ratio[layer] * nearer
            solved[layer, :, lanes] = nearer.astype(solved.dtype)


def chain_solve(target, coefficients):
    return pl.pallas_call(
        solve_kernel,
        out_shape=jax.ShapeDtypeStruct(target.shape, BF16),
        compiler_params=pltpu.CompilerParams(vmem_limit_bytes=32 * 2**20),
        name="chain_solve",
    )(target, *coefficients)


def by_layer(value):
    return lax.all_to_all(value, LAYER, 0, 0)


def block_diagonal(block):
    return jnp.sum(jnp.where(jnp.eye(block.shape[0], dtype=bool), block, 0.0), axis=0)


def body(activations, factor_old, cross_old, gradients, moments, exponents, master):
    acts, factor_old, cross_old, grad = activations[0], factor_old[0], cross_old[0], gradients[0]
    rows, features = factor_old.shape
    outputs = grad.shape[1]
    slim = rows // LAYERS
    place = lax.axis_index(DP)
    start = place * rows
    weight = (1.0 - FACTOR_DECAY) / (rows * GROUP)
    order = piece_order()

    half = acts.shape[0] // 2
    above = along_layers(acts[:half], -1).astype(F32)
    below = along_layers(acts[half:], 1).astype(F32)
    wide = acts.astype(F32)
    squares = jnp.sum(wide * wide, axis=0)
    with_above = jnp.sum(wide[:half] * above, axis=0)
    with_below = jnp.sum(wide[half:] * below, axis=0)
    old_diagonals = jnp.stack(
        [
            block_diagonal(lax.dynamic_slice_in_dim(factor_old, start, rows, 1)),
            block_diagonal(lax.dynamic_slice_in_dim(cross_old, start, rows, 1)),
            jnp.zeros((rows,), F32),
        ]
    )
    sums = (weight * jnp.stack([squares, with_above, with_below])).reshape(3, GROUP, rows)
    here = (jnp.arange(GROUP) == place)[None, :, None]
    sums = sums + jnp.where(here, FACTOR_DECAY * old_diagonals[:, None, :], 0.0)
    message = sums.reshape(3, GROUP, LAYERS, slim).transpose(2, 1, 0, 3).reshape(LAYERS * GROUP, 3 * slim)
    message = jnp.pad(message, ((0, 0), (0, 128 - 3 * slim)))
    arrived = lax.all_to_all(message, LAYER + DP, 0, 0, tiled=True)
    diagonals = jnp.sum(arrived.reshape(LAYERS, GROUP, 128), axis=1)[:, : 3 * slim].reshape(LAYERS, 3, slim)
    pivots = DAMPING + diagonals[:, 0]
    coupling = diagonals[:, 1] + jnp.concatenate([diagonals[1:, 2], jnp.zeros((1, slim), F32)], 0)
    inverse = 1.0 / pivots
    coefficients = [
        jnp.broadcast_to(c[:, :, None], (LAYERS, slim, 128)) for c in (inverse, coupling, coupling * inverse)
    ]

    initial_rows = chain_solve(by_layer(grad.reshape(LAYERS, slim, outputs)), coefficients)
    initial = by_layer(initial_rows).reshape(rows, outputs)

    pieces = gathered(acts)
    own = lax.all_to_all(acts.reshape(rows, GROUP, rows), DP, 1, 0)
    lower = along_layers(own, 1)
    upper = along_layers(own, -1)
    cross_slim = cross_old.astype(BF16)
    row_old = along_layers(cross_slim, 1)
    col_old = lax.all_to_all(cross_slim.reshape(rows, GROUP, rows), DP, 1, 0)
    factor_new, factor_hi, factor_lo, row_hi, row_lo, row_batch, col_hi, col_lo = refresh(
        weight, order, pieces, own, lower, upper, factor_old, row_old, col_old
    )
    cross_new = FACTOR_DECAY * cross_old + weight * along_layers(row_batch, -1).astype(F32)

    solution_pieces = gathered(initial)
    rest, down, up = apply_blocks(
        order, solution_pieces, (factor_hi, factor_lo, row_hi, row_lo, col_hi, col_lo), grad
    )
    rest = rest - along_layers(down, -1).astype(F32) - along_layers(up, 1).astype(F32)
    change_rows = chain_solve(by_layer(rest.astype(BF16).reshape(LAYERS, slim, outputs)), coefficients)
    change = by_layer(change_rows).reshape(rows, outputs)
    update = initial.astype(F32) + change.astype(F32)

    dequant = jnp.repeat(jnp.exp2(exponents[0].astype(F32)), SCALE_BLOCK)[:, None]
    requant = jnp.repeat(jnp.exp2(-exponents[0].astype(F32)), SCALE_BLOCK)[:, None]
    moment = MOMENTUM * moments[0].astype(F32) * dequant + (1.0 - MOMENTUM) * update
    moments_new = (moment * requant).astype(BF16)
    master_new = master[0] - STEP_SIZE * moment
    replicas = jnp.zeros((GROUP, rows, outputs), BF16)
    for k, piece in enumerate(gathered(master_new.astype(BF16))):
        replicas = lax.dynamic_update_index_in_dim(replicas, piece, order[k], 0)
    replicas = replicas.reshape(features, outputs)
    return (factor_new[None], cross_new[None], moments_new[None], master_new[None], replicas[None])


def solution(mesh):
    finer = Mesh(mesh.devices.reshape(2, 4, 2, 2, TURN), LAYER + DP)
    sharded = P(LAYER, DP, None)
    in_specs = (sharded,) * 5 + (P(LAYER, DP), sharded)
    out_specs = (sharded,) * 4 + (P(LAYER, None, None),)
    return jax.shard_map(body, mesh=finer, in_specs=in_specs, out_specs=out_specs, check_vma=False)
```

```python
import jax
import jax.numpy as jnp
from jax import lax
from jax.experimental import pallas as pl
from jax.experimental.pallas import tpu as pltpu
from jax.sharding import Mesh
from jax.sharding import PartitionSpec as P

SCALE_BLOCK = 128
LAYER = ("layer_0", "layer_1", "layer_2")
DP = ("dp_0", "dp_1")
LAYERS = 16
GROUP = 8
TURN = 4

FACTOR_DECAY = 0.9
DAMPING = 0.5
MOMENTUM = 0.8
STEP_SIZE = 0.05

F32 = jnp.float32
BF16 = jnp.bfloat16


def along_layers(value, steps):
    pairs = [(i, i + steps) for i in range(LAYERS) if 0 <= i + steps < LAYERS]
    return lax.ppermute(value, LAYER, pairs)


def turned(value, steps):
    return lax.ppermute(value, "dp_1", [(i, (i + steps) % TURN) for i in range(TURN)])


def across(value):
    return lax.ppermute(value, "dp_0", [(0, 1), (1, 0)])


def first_round(own):
    return across(own), turned(own, 1), turned(own, 3)


def second_round(other, before, after):
    return turned(other, 1), across(after), turned(after, 3)


def third_round(other_before, other_after):
    half = other_before.shape[0] // 2
    return jnp.concatenate([turned(other_before[:half], 1), turned(other_after[half:], 3)], 0)


def gathered(own):
    other, before, after = first_round(own)
    other_before, other_after, far = second_round(other, before, after)
    return (own, before, after, other, other_before, other_after, far, third_round(other_before, other_after))


def piece_order():
    mine, turn = lax.axis_index("dp_0"), lax.axis_index("dp_1")
    side = jnp.stack([mine, mine, mine] + [1 - mine] * 3 + [mine, 1 - mine])
    steps = jnp.array([0, 3, 1, 0, 3, 1, 2, 2], jnp.int32)
    return (side * TURN + (turn + steps) % TURN).astype(jnp.int32)


def after(value, *others):
    return lax.optimization_barrier((value, others))[0]


def transposed_dot(left, right):
    return lax.dot_general(left, right, (((0,), (0,)), ((), ())), preferred_element_type=F32)


def refresh_kernel(weight, order, *refs):
    pieces, columns, (factor_old, row_old, col_old) = refs[:GROUP], refs[GROUP : GROUP + 9], refs[GROUP + 9 : GROUP + 12]
    factor, factor_off, row_batch, row_off, col_off = refs[GROUP + 12 :]
    own, lower, upper = columns[:3], columns[3:6], columns[6:]
    sums = [None, None, None]
    for k in range(GROUP):
        right = pieces[k][...]
        for n, parts in enumerate((own, lower, upper)):
            stage = 0 if k < 4 else 1 if k < 7 else 2
            left = parts[stage][k - (0, 4, 7)[stage]]
            part = transposed_dot(left, right)
            sums[n] = part if k == 0 else sums[n] + part
    rows, tile = factor.shape
    column = pl.program_id(0) * tile + lax.broadcasted_iota(jnp.int32, (rows, tile), 1)
    diagonal = column == order[0] * rows + lax.broadcasted_iota(jnp.int32, (rows, tile), 0)
    fresh = FACTOR_DECAY * factor_old[...] + weight * sums[0]
    factor[...] = fresh
    factor_off[...] = jnp.where(diagonal, 0.0, fresh).astype(BF16)
    row_batch[...] = sums[1].astype(BF16)
    row = FACTOR_DECAY * row_old[...].astype(F32) + weight * sums[1]
    row_off[...] = jnp.where(diagonal, 0.0, row).astype(BF16)
    old = jnp.concatenate([col_old[b].astype(F32).T for b in range(col_old.shape[0])], 1)
    col_off[...] = jnp.where(diagonal, 0.0, FACTOR_DECAY * old + weight * sums[2]).astype(BF16)


def refresh(weight, order, pieces, columns, factor_old, row_old, col_old):
    rows, features = factor_old.shape
    tile = 512
    blocks = tile // rows
    column = pl.BlockSpec((rows, tile), lambda j, o: (0, j))
    stacked = pl.BlockSpec((blocks, rows, rows), lambda j, o: (j, 0, 0))
    kinds = (F32, BF16, BF16, BF16, BF16)
    return pl.pallas_call(
        lambda *refs: refresh_kernel(weight, *refs),
        grid_spec=pltpu.PrefetchScalarGridSpec(
            num_scalar_prefetch=1,
            grid=(features // tile,),
            in_specs=[column] * GROUP
            + [pl.BlockSpec(c.shape, lambda j, o: (0, 0, 0)) for c in columns]
            + [column, column, stacked],
            out_specs=[column] * len(kinds),
        ),
        out_shape=[jax.ShapeDtypeStruct((rows, features), kind) for kind in kinds],
        compiler_params=pltpu.CompilerParams(vmem_limit_bytes=48 * 2**20),
        name="refresh",
    )(order, *pieces, *columns, factor_old, row_old, col_old)


def apply_kernel(order, *refs):
    pieces, matrices, (out, joined) = refs[:GROUP], refs[GROUP : GROUP + 3], refs[GROUP + 3 :]
    rows = pieces[0].shape[0]
    for k in range(GROUP):
        joined[pl.ds(pl.multiple_of(order[k] * rows, rows), rows), :] = pieces[k][...]
    full = joined[...]
    slim = rows // LAYERS
    for n, matrix in enumerate(matrices):
        product = jnp.dot(matrix[...], full, preferred_element_type=F32).astype(BF16)
        for layer in range(LAYERS):
            out[layer, n * slim : (n + 1) * slim, :] = product[layer * slim : (layer + 1) * slim]


def apply_blocks(order, pieces, matrices):
    rows, outputs = pieces[0].shape
    features = matrices[0].shape[1]
    tile = 512
    slim = rows // LAYERS
    return pl.pallas_call(
        apply_kernel,
        grid_spec=pltpu.PrefetchScalarGridSpec(
            num_scalar_prefetch=1,
            grid=(outputs // tile,),
            in_specs=[pl.BlockSpec((rows, tile), lambda j, o: (0, j))] * GROUP
            + [pl.BlockSpec((rows, features), lambda j, o: (0, 0))] * 3,
            out_specs=pl.BlockSpec((LAYERS, 3 * slim, tile), lambda j, o: (0, 0, j)),
            scratch_shapes=[pltpu.VMEM((features, tile), BF16)],
        ),
        out_shape=jax.ShapeDtypeStruct((LAYERS, 3 * slim, outputs), BF16),
        compiler_params=pltpu.CompilerParams(vmem_limit_bytes=48 * 2**20),
        name="apply_blocks",
    )(order, *pieces, *matrices)


def sweep(target, inverse, coupling, ratio, store):
    passed = jnp.zeros_like(target[0])
    scaled = []
    for layer in range(LAYERS):
        scaled.append((target[layer] - passed) * inverse[layer])
        passed = coupling[layer] * scaled[layer]
    nearer = jnp.zeros_like(passed)
    for layer in reversed(range(LAYERS)):
        nearer = scaled[layer] - ratio[layer] * nearer
        store(layer, nearer)


def initial_kernel(grad, pivots, inverse, coupling, ratio, solved):
    for start in range(0, grad.shape[-1], 128):
        lanes = pl.ds(start, 128)

        def store(layer, value):
            solved[layer, :, lanes] = value.astype(solved.dtype)

        sweep([grad[layer, :, lanes].astype(F32) for layer in range(LAYERS)], inverse, coupling, ratio, store)


def change_kernel(grad, initial, off, pivots, inverse, coupling, ratio, solved):
    slim = grad.shape[1]
    for start in range(0, grad.shape[-1], 128):
        lanes = pl.ds(start, 128)
        first = [initial[layer, :, lanes].astype(F32) for layer in range(LAYERS)]
        target = []
        for layer in range(LAYERS):
            applied = pivots[layer] * first[layer] + off[layer, :slim, lanes].astype(F32)
            if layer + 1 < LAYERS:
                applied = applied + coupling[layer] * first[layer + 1]
                applied = applied + off[layer + 1, 2 * slim : 3 * slim, lanes].astype(F32)
            if layer > 0:
                applied = applied + coupling[layer - 1] * first[layer - 1]
                applied = applied + off[layer - 1, slim : 2 * slim, lanes].astype(F32)
            target.append(grad[layer, :, lanes].astype(F32) - applied)

        def store(layer, value):
            solved[layer, :, lanes] = value.astype(solved.dtype)

        sweep(target, inverse, coupling, ratio, store)


def chain_solve(kernel, name, arrays, coefficients):
    return pl.pallas_call(
        kernel,
        out_shape=jax.ShapeDtypeStruct(arrays[0].shape, BF16),
        compiler_params=pltpu.CompilerParams(vmem_limit_bytes=32 * 2**20),
        name=name,
    )(*arrays, *coefficients)


def by_layer(value):
    return lax.all_to_all(value, LAYER, 0, 0)


def block_diagonal(block):
    return jnp.sum(jnp.where(jnp.eye(block.shape[0], dtype=bool), block, 0.0), axis=0)


def body(activations, factor_old, cross_old, gradients, moments, exponents, master):
    acts, factor_old, cross_old, grad = activations[0], factor_old[0], cross_old[0], gradients[0]
    rows, features = factor_old.shape
    outputs = grad.shape[1]
    slim = rows // LAYERS
    place = lax.axis_index(DP)
    start = place * rows
    weight = (1.0 - FACTOR_DECAY) / (rows * GROUP)
    order = piece_order()

    half = acts.shape[0] // 2
    above = along_layers(acts[:half], -1).astype(F32)
    below = along_layers(acts[half:], 1).astype(F32)
    wide = acts.astype(F32)
    squares = jnp.sum(wide * wide, axis=0)
    with_above = jnp.sum(wide[:half] * above, axis=0)
    with_below = jnp.sum(wide[half:] * below, axis=0)
    old_diagonals = jnp.stack(
        [
            block_diagonal(lax.dynamic_slice_in_dim(factor_old, start, rows, 1)),
            block_diagonal(lax.dynamic_slice_in_dim(cross_old, start, rows, 1)),
            jnp.zeros((rows,), F32),
        ]
    )
    sums = (weight * jnp.stack([squares, with_above, with_below])).reshape(3, GROUP, rows)
    here = (jnp.arange(GROUP) == place)[None, :, None]
    sums = sums + jnp.where(here, FACTOR_DECAY * old_diagonals[:, None, :], 0.0)
    message = sums.reshape(3, GROUP, LAYERS, slim).transpose(2, 1, 0, 3).reshape(LAYERS * GROUP, 3 * slim)
    grad_rows = by_layer(grad.reshape(LAYERS, slim, outputs))
    message = after(jnp.pad(message, ((0, 0), (0, 128 - 3 * slim))), grad_rows)
    other, before, beyond = first_round(acts)
    arrived = after(lax.all_to_all(message, LAYER + DP, 0, 0, tiled=True), other, before, beyond)
    diagonals = jnp.sum(arrived.reshape(LAYERS, GROUP, 128), axis=1)[:, : 3 * slim].reshape(LAYERS, 3, slim)
    pivots = DAMPING + diagonals[:, 0]
    coupling = diagonals[:, 1] + jnp.concatenate([diagonals[1:, 2], jnp.zeros((1, slim), F32)], 0)
    inverse = 1.0 / pivots
    coefficients = [
        jnp.broadcast_to(c[:, :, None], (LAYERS, slim, 128))
        for c in (pivots, inverse, coupling, coupling * inverse)
    ]

    def own_columns(parts):
        mine = jnp.stack([lax.dynamic_slice_in_dim(part, start, rows, 1) for part in parts])
        return mine, along_layers(mine, 1), along_layers(mine, -1)

    columns = [own_columns((acts, before, beyond, other))]
    other_before, other_beyond, far = second_round(other, before, beyond)
    columns.append(own_columns((other_before, other_beyond, far)))

    initial_rows = chain_solve(initial_kernel, "first_solution", (grad_rows,), coefficients)
    initial = by_layer(initial_rows).reshape(rows, outputs)
    initial = after(initial, other_before, other_beyond, far)

    other_far = third_round(other_before, other_beyond)
    columns.append(own_columns((other_far,)))
    pieces = (acts, before, beyond, other, other_before, other_beyond, far, other_far)
    columns = [stage[n] for n in range(3) for stage in columns]
    cross_slim = cross_old.astype(BF16)
    row_old = along_layers(cross_slim, 1)
    col_old = lax.all_to_all(cross_slim.reshape(rows, GROUP, rows), DP, 1, 0)
    factor_new, factor_off, row_batch, row_off, col_off = refresh(
        weight, order, pieces, columns, factor_old, row_old, col_old
    )
    cross_new = FACTOR_DECAY * cross_old + weight * along_layers(row_batch, -1).astype(F32)

    off = apply_blocks(order, gathered(initial), (factor_off, col_off, row_off))
    change_rows = chain_solve(change_kernel, "change", (grad_rows, initial_rows, by_layer(off)), coefficients)
    change = by_layer(change_rows).reshape(rows, outputs)
    update = initial.astype(F32) + change.astype(F32)

    dequant = jnp.repeat(jnp.exp2(exponents[0].astype(F32)), SCALE_BLOCK)[:, None]
    requant = jnp.repeat(jnp.exp2(-exponents[0].astype(F32)), SCALE_BLOCK)[:, None]
    moment = MOMENTUM * moments[0].astype(F32) * dequant + (1.0 - MOMENTUM) * update
    moments_new = (moment * requant).astype(BF16)
    master_new = master[0] - STEP_SIZE * moment
    replicas = jnp.zeros((GROUP, rows, outputs), BF16)
    for k, piece in enumerate(gathered(master_new.astype(BF16))):
        replicas = lax.dynamic_update_index_in_dim(replicas, piece, order[k], 0)
    replicas = replicas.reshape(features, outputs)
    return (factor_new[None], cross_new[None], moments_new[None], master_new[None], replicas[None])


def solution(mesh):
    finer = Mesh(mesh.devices.reshape(2, 4, 2, 2, TURN), LAYER + DP)
    sharded = P(LAYER, DP, None)
    in_specs = (sharded,) * 5 + (P(LAYER, DP), sharded)
    out_specs = (sharded,) * 4 + (P(LAYER, None, None),)
    return jax.shard_map(body, mesh=finer, in_specs=in_specs, out_specs=out_specs, check_vma=False)
```

```python
import jax
import jax.numpy as jnp
from jax import lax
from jax.experimental import pallas as pl
from jax.experimental.pallas import tpu as pltpu
from jax.sharding import Mesh
from jax.sharding import PartitionSpec as P

SCALE_BLOCK = 128
LAYER = ("layer_0", "layer_1", "layer_2")
DP = ("dp_0", "dp_1")
LAYERS = 16
GROUP = 8
TURN = 4

FACTOR_DECAY = 0.9
DAMPING = 0.5
MOMENTUM = 0.8
STEP_SIZE = 0.05

F32 = jnp.float32
BF16 = jnp.bfloat16


def along_layers(value, steps):
    pairs = [(i, i + steps) for i in range(LAYERS) if 0 <= i + steps < LAYERS]
    return lax.ppermute(value, LAYER, pairs)


def turned(value, steps):
    return lax.ppermute(value, "dp_1", [(i, (i + steps) % TURN) for i in range(TURN)])


def across(value):
    return lax.ppermute(value, "dp_0", [(0, 1), (1, 0)])


def first_round(own):
    return across(own), turned(own, 1), turned(own, 3), turned(own, 2)


def second_round(other, far):
    return turned(other, 1), turned(other, 3), across(far)


def gathered(own):
    other, before, beyond, far = tied(*first_round(own))
    return own, before, beyond, other, far, *second_round(other, far)


def piece_order():
    mine, turn = lax.axis_index("dp_0"), lax.axis_index("dp_1")
    side = jnp.stack([mine] * 3 + [1 - mine, mine] + [1 - mine] * 3)
    steps = jnp.array([0, 3, 1, 0, 2, 3, 1, 2], jnp.int32)
    return (side * TURN + (turn + steps) % TURN).astype(jnp.int32)


def tied(*values):
    return lax.optimization_barrier(values)


def transposed_dot(left, right):
    return lax.dot_general(left, right, (((0,), (0,)), ((), ())), preferred_element_type=F32)


def pick_kernel(order, *refs):
    for k, piece in enumerate(refs[:-1]):
        refs[-1][k] = piece[...]


def own_columns(order, pieces):
    rows = pieces[0].shape[0]
    return pl.pallas_call(
        pick_kernel,
        grid_spec=pltpu.PrefetchScalarGridSpec(
            num_scalar_prefetch=1,
            grid=(1,),
            in_specs=[pl.BlockSpec((rows, rows), lambda j, o: (0, o[0]))] * len(pieces),
            out_specs=pl.BlockSpec((len(pieces), rows, rows), lambda j, o: (0, 0, 0)),
        ),
        out_shape=jax.ShapeDtypeStruct((len(pieces), rows, rows), pieces[0].dtype),
        name="own_columns",
    )(order, *pieces)


def refresh_kernel(weight, order, *refs):
    pieces, columns, (factor_old, row_old) = refs[:GROUP], refs[GROUP : GROUP + 3], refs[GROUP + 3 : GROUP + 5]
    factor, factor_off, row_batch, row_off, col_off = refs[GROUP + 5 :]
    sums = [None, None, None]
    for k in range(GROUP):
        right = pieces[k][...]
        for n in range(3):
            part = transposed_dot(columns[n][k], right)
            sums[n] = part if k == 0 else sums[n] + part
    rows, tile = factor.shape
    column = pl.program_id(0) * tile + lax.broadcasted_iota(jnp.int32, (rows, tile), 1)
    diagonal = column == order[0] * rows + lax.broadcasted_iota(jnp.int32, (rows, tile), 0)
    fresh = FACTOR_DECAY * factor_old[...] + weight * sums[0]
    factor[...] = fresh
    factor_off[...] = jnp.where(diagonal, 0.0, fresh).astype(BF16)
    row_batch[...] = sums[1].astype(BF16)
    row = FACTOR_DECAY * row_old[...].astype(F32) + weight * sums[1]
    row_off[...] = jnp.where(diagonal, 0.0, row).astype(BF16)
    col_off[...] = jnp.where(diagonal, 0.0, weight * sums[2]).astype(BF16)


def refresh(weight, order, pieces, columns, factor_old, row_old):
    rows, features = factor_old.shape
    tile = 512
    column = pl.BlockSpec((rows, tile), lambda j, o: (0, j))
    kinds = (F32, BF16, BF16, BF16, BF16)
    return pl.pallas_call(
        lambda *refs: refresh_kernel(weight, *refs),
        grid_spec=pltpu.PrefetchScalarGridSpec(
            num_scalar_prefetch=1,
            grid=(features // tile,),
            in_specs=[column] * GROUP
            + [pl.BlockSpec(c.shape, lambda j, o: (0, 0, 0)) for c in columns]
            + [column, column],
            out_specs=[column] * len(kinds),
        ),
        out_shape=[jax.ShapeDtypeStruct((rows, features), kind) for kind in kinds],
        compiler_params=pltpu.CompilerParams(vmem_limit_bytes=48 * 2**20),
        name="refresh",
    )(order, *pieces, *columns, factor_old, row_old)


def place_kernel(order, *refs):
    count = order.shape[0]
    for k in range(count):
        @pl.when(pl.program_id(0) == k)
        def _():
            refs[-1][...] = refs[k][...]


def place_rows(order, pieces, base):
    rows, outputs = pieces[0].shape
    arrays = list(pieces) + ([] if base is None else [base])
    return pl.pallas_call(
        place_kernel,
        grid_spec=pltpu.PrefetchScalarGridSpec(
            num_scalar_prefetch=1,
            grid=(len(pieces),),
            in_specs=[pl.BlockSpec((rows, outputs), lambda j, o: (0, 0))] * len(pieces)
            + [pl.BlockSpec(memory_space=pl.ANY)] * (len(arrays) - len(pieces)),
            out_specs=pl.BlockSpec((rows, outputs), lambda j, o: (o[j], 0)),
        ),
        out_shape=jax.ShapeDtypeStruct((GROUP * rows, outputs), pieces[0].dtype),
        input_output_aliases={} if base is None else {len(arrays): 0},
        name="place_rows",
    )(order, *arrays)


def apply_kernel(order, *refs):
    pieces, matrices, (col_old, out, joined) = refs[:GROUP], refs[GROUP : GROUP + 3], refs[GROUP + 3 :]
    rows = pieces[0].shape[0]
    for k in range(GROUP):
        joined[pl.ds(pl.multiple_of(order[k] * rows, rows), rows), :] = pieces[k][...]
    full = joined[...]
    slim = rows // LAYERS
    diagonal = lax.broadcasted_iota(jnp.int32, (rows, rows), 0) == lax.broadcasted_iota(jnp.int32, (rows, rows), 1)
    old = None
    for k in range(GROUP):
        block = col_old[order[k]]
        block = jnp.where(diagonal, jnp.zeros_like(block), block) if k == 0 else block
        part = transposed_dot(block, pieces[k][...])
        old = part if k == 0 else old + part
    for n, matrix in enumerate(matrices):
        product = jnp.dot(matrix[...], full, preferred_element_type=F32)
        product = (product + FACTOR_DECAY * old if n == 1 else product).astype(BF16)
        for layer in range(LAYERS):
            out[layer, n * slim : (n + 1) * slim, :] = product[layer * slim : (layer + 1) * slim]


def apply_blocks(order, pieces, matrices, col_old):
    rows, outputs = pieces[0].shape
    features = matrices[0].shape[1]
    tile = 512
    slim = rows // LAYERS
    return pl.pallas_call(
        apply_kernel,
        grid_spec=pltpu.PrefetchScalarGridSpec(
            num_scalar_prefetch=1,
            grid=(outputs // tile,),
            in_specs=[pl.BlockSpec((rows, tile), lambda j, o: (0, j))] * GROUP
            + [pl.BlockSpec((rows, features), lambda j, o: (0, 0))] * 3
            + [pl.BlockSpec((GROUP, rows, rows), lambda j, o: (0, 0, 0))],
            out_specs=pl.BlockSpec((LAYERS, 3 * slim, tile), lambda j, o: (0, 0, j)),
            scratch_shapes=[pltpu.VMEM((features, tile), BF16)],
        ),
        out_shape=jax.ShapeDtypeStruct((LAYERS, 3 * slim, outputs), BF16),
        compiler_params=pltpu.CompilerParams(vmem_limit_bytes=48 * 2**20),
        name="apply_blocks",
    )(order, *pieces, *matrices, col_old)


def sweep(target, inverse, coupling, ratio, store):
    passed = jnp.zeros_like(target[0])
    scaled = []
    for layer in range(LAYERS):
        scaled.append((target[layer] - passed) * inverse[layer])
        passed = coupling[layer] * scaled[layer]
    nearer = jnp.zeros_like(passed)
    for layer in reversed(range(LAYERS)):
        nearer = scaled[layer] - ratio[layer] * nearer
        store(layer, nearer)


def initial_kernel(grad, pivots, inverse, coupling, ratio, solved):
    for start in range(0, grad.shape[-1], 128):
        lanes = pl.ds(start, 128)

        def store(layer, value):
            solved[layer, :, lanes] = value.astype(solved.dtype)

        sweep([grad[layer, :, lanes].astype(F32) for layer in range(LAYERS)], inverse, coupling, ratio, store)


def change_kernel(grad, initial, off, pivots, inverse, coupling, ratio, solved):
    slim = grad.shape[1]
    for start in range(0, grad.shape[-1], 128):
        lanes = pl.ds(start, 128)
        first = [initial[layer, :, lanes].astype(F32) for layer in range(LAYERS)]
        target = []
        for layer in range(LAYERS):
            applied = pivots[layer] * first[layer] + off[layer, :slim, lanes].astype(F32)
            if layer + 1 < LAYERS:
                applied = applied + coupling[layer] * first[layer + 1]
                applied = applied + off[layer + 1, 2 * slim : 3 * slim, lanes].astype(F32)
            if layer > 0:
                applied = applied + coupling[layer - 1] * first[layer - 1]
                applied = applied + off[layer - 1, slim : 2 * slim, lanes].astype(F32)
            target.append(grad[layer, :, lanes].astype(F32) - applied)

        def store(layer, value):
            solved[layer, :, lanes] = value.astype(solved.dtype)

        sweep(target, inverse, coupling, ratio, store)


def chain_solve(kernel, name, arrays, coefficients):
    return pl.pallas_call(
        kernel,
        out_shape=jax.ShapeDtypeStruct(arrays[0].shape, BF16),
        compiler_params=pltpu.CompilerParams(vmem_limit_bytes=32 * 2**20),
        name=name,
    )(*arrays, *coefficients)


def by_layer(value):
    return lax.all_to_all(value, LAYER, 0, 0)


def block_diagonal(block):
    return jnp.sum(jnp.where(jnp.eye(block.shape[0], dtype=bool), block, 0.0), axis=0)


def body(activations, factor_old, cross_old, gradients, moments, exponents, master):
    acts, factor_old, cross_old, grad = activations[0], factor_old[0], cross_old[0], gradients[0]
    rows, features = factor_old.shape
    outputs = grad.shape[1]
    slim = rows // LAYERS
    place = lax.axis_index(DP)
    start = place * rows
    weight = (1.0 - FACTOR_DECAY) / (rows * GROUP)
    order = piece_order()

    above = along_layers(acts, -1)
    before, beyond = turned(acts, 1), turned(acts, 3)
    grad_rows = by_layer(grad.reshape(LAYERS, slim, outputs))
    cross_blocks = cross_old.astype(BF16).reshape(rows, GROUP, rows).transpose(1, 0, 2)
    wide = acts.astype(F32)
    sums = jnp.stack([jnp.sum(wide * wide, axis=0), jnp.sum(wide * above.astype(F32), axis=0)])
    old_diagonals = jnp.stack(
        [block_diagonal(lax.dynamic_slice_in_dim(old, start, rows, 1)) for old in (factor_old, cross_old)]
    )
    here = (jnp.arange(GROUP) == place)[None, :, None]
    sums = weight * sums.reshape(2, GROUP, rows) + jnp.where(here, FACTOR_DECAY * old_diagonals[:, None, :], 0.0)
    message = sums.reshape(2, GROUP, LAYERS, slim).transpose(2, 1, 0, 3).reshape(LAYERS * GROUP, 2 * slim)
    message = jnp.pad(message, ((0, 0), (0, 128 - 2 * slim)))
    message, grad_rows, cross_blocks, shard, before, beyond = tied(
        message, grad_rows, cross_blocks, acts, before, beyond
    )
    other = across(shard)
    far = turned(before, 1)
    arrived = lax.all_to_all(message, LAYER + DP, 0, 0, tiled=True)
    arrived, other, far = tied(arrived, other, far)
    diagonals = jnp.sum(arrived.reshape(LAYERS, GROUP, 128), axis=1)[:, : 2 * slim].reshape(LAYERS, 2, slim)
    coupling = diagonals[:, 1]
    pivots = DAMPING + diagonals[:, 0]
    inverse = 1.0 / pivots
    coefficients = [
        jnp.broadcast_to(c[:, :, None], (LAYERS, slim, 128))
        for c in (pivots, inverse, coupling, coupling * inverse)
    ]

    initial_rows = chain_solve(initial_kernel, "first_solution", (grad_rows,), coefficients)
    initial_rows, other, far = tied(initial_rows, other, far)
    initial = by_layer(initial_rows).reshape(rows, outputs)

    remote = (far, turned(other, 1), turned(other, 3), across(far))
    initial, cross_slim, cross_blocks, *remote = tied(initial, cross_old.astype(BF16), cross_blocks, *remote)
    pieces = (shard, before, beyond, other, *remote)
    own = own_columns(order, pieces)
    columns = (own, along_layers(own, 1), along_layers(own, -1))
    row_old = along_layers(cross_slim, 1)
    col_old = lax.all_to_all(cross_blocks, DP, 0, 0, tiled=True)
    factor_new, factor_off, row_batch, row_off, col_off = refresh(
        weight, order, pieces, columns, factor_old, row_old
    )
    off = apply_blocks(order, gathered(initial), (factor_off, col_off, row_off), col_old)
    change_rows = chain_solve(change_kernel, "change", (grad_rows, initial_rows, by_layer(off)), coefficients)
    change = by_layer(change_rows).reshape(rows, outputs)
    update = initial.astype(F32) + change.astype(F32)

    dequant = jnp.repeat(jnp.exp2(exponents[0].astype(F32)), SCALE_BLOCK)[:, None]
    requant = jnp.repeat(jnp.exp2(-exponents[0].astype(F32)), SCALE_BLOCK)[:, None]
    moment = MOMENTUM * moments[0].astype(F32) * dequant + (1.0 - MOMENTUM) * update
    moments_new = (moment * requant).astype(BF16)
    master_new = master[0] - STEP_SIZE * moment
    own = master_new.astype(BF16)
    other, before, beyond, far = first_round(own)
    other, row_batch = tied(other, row_batch)
    cross_new = FACTOR_DECAY * cross_old + weight * along_layers(row_batch, -1).astype(F32)
    replicas = place_rows(order[:5], (own, before, beyond, other, far), None)
    replicas, cross_new = tied(replicas, cross_new)
    replicas = place_rows(order[5:], second_round(other, far), replicas)
    return (factor_new[None], cross_new[None], moments_new[None], master_new[None], replicas[None])


def solution(mesh):
    finer = Mesh(mesh.devices.reshape(2, 4, 2, 2, TURN), LAYER + DP)
    sharded = P(LAYER, DP, None)
    in_specs = (sharded,) * 5 + (P(LAYER, DP), sharded)
    out_specs = (sharded,) * 4 + (P(LAYER, None, None),)
    return jax.shard_map(body, mesh=finer, in_specs=in_specs, out_specs=out_specs, check_vma=False)
```

```python
import jax
import jax.numpy as jnp
from jax import lax
from jax.experimental import pallas as pl
from jax.experimental.pallas import tpu as pltpu
from jax.sharding import Mesh
from jax.sharding import PartitionSpec as P

SCALE_BLOCK = 128
LAYER = ("layer_0", "layer_1", "layer_2")
DP = ("dp_0", "dp_1")
LAYERS = 16
GROUP = 8
TURN = 4

FACTOR_DECAY = 0.9
DAMPING = 0.5
MOMENTUM = 0.8
STEP_SIZE = 0.05

F32 = jnp.float32
BF16 = jnp.bfloat16


def along_layers(value, steps):
    pairs = [(i, i + steps) for i in range(LAYERS) if 0 <= i + steps < LAYERS]
    return lax.ppermute(value, LAYER, pairs)


def turned(value, steps):
    return lax.ppermute(value, "dp_1", [(i, (i + steps) % TURN) for i in range(TURN)])


def across(value):
    return lax.ppermute(value, "dp_0", [(0, 1), (1, 0)])


def first_round(own):
    return across(own), turned(own, 1), turned(own, 3), turned(own, 2)


def second_round(other, far):
    return turned(other, 1), turned(other, 3), across(far)


def gathered(own):
    other, before, beyond, far = tied(*first_round(own))
    return own, before, beyond, other, far, *second_round(other, far)


def piece_order():
    mine, turn = lax.axis_index("dp_0"), lax.axis_index("dp_1")
    side = jnp.stack([mine] * 3 + [1 - mine, mine] + [1 - mine] * 3)
    steps = jnp.array([0, 3, 1, 0, 2, 3, 1, 2], jnp.int32)
    return (side * TURN + (turn + steps) % TURN).astype(jnp.int32)


def tied(*values):
    return lax.optimization_barrier(values)


def transposed_dot(left, right):
    return lax.dot_general(left, right, (((0,), (0,)), ((), ())), preferred_element_type=F32)


def pick_kernel(order, *refs):
    for k, piece in enumerate(refs[:-1]):
        refs[-1][k] = piece[...]


def own_columns(order, pieces):
    rows = pieces[0].shape[0]
    return pl.pallas_call(
        pick_kernel,
        grid_spec=pltpu.PrefetchScalarGridSpec(
            num_scalar_prefetch=1,
            grid=(1,),
            in_specs=[pl.BlockSpec((rows, rows), lambda j, o: (0, o[0]))] * len(pieces),
            out_specs=pl.BlockSpec((len(pieces), rows, rows), lambda j, o: (0, 0, 0)),
        ),
        out_shape=jax.ShapeDtypeStruct((len(pieces), rows, rows), pieces[0].dtype),
        name="own_columns",
    )(order, *pieces)


def refresh_kernel(weight, order, *refs):
    pieces, columns, (factor_old, row_old) = refs[:GROUP], refs[GROUP : GROUP + 3], refs[GROUP + 3 : GROUP + 5]
    factor, factor_off, row_batch, row_off, col_off = refs[GROUP + 5 :]
    sums = [None, None, None]
    for k in range(GROUP):
        right = pieces[k][...]
        for n in range(3):
            part = transposed_dot(columns[n][k], right)
            sums[n] = part if k == 0 else sums[n] + part
    rows, tile = factor.shape
    column = pl.program_id(0) * tile + lax.broadcasted_iota(jnp.int32, (rows, tile), 1)
    diagonal = column == order[0] * rows + lax.broadcasted_iota(jnp.int32, (rows, tile), 0)
    fresh = FACTOR_DECAY * factor_old[...] + weight * sums[0]
    factor[...] = fresh
    factor_off[...] = jnp.where(diagonal, 0.0, fresh).astype(BF16)
    row_batch[...] = sums[1].astype(BF16)
    row = FACTOR_DECAY * row_old[...].astype(F32) + weight * sums[1]
    row_off[...] = jnp.where(diagonal, 0.0, row).astype(BF16)
    col_off[...] = jnp.where(diagonal, 0.0, weight * sums[2]).astype(BF16)


def refresh(weight, order, pieces, columns, factor_old, row_old):
    rows, features = factor_old.shape
    tile = 512
    column = pl.BlockSpec((rows, tile), lambda j, o: (0, j))
    kinds = (F32, BF16, BF16, BF16, BF16)
    return pl.pallas_call(
        lambda *refs: refresh_kernel(weight, *refs),
        grid_spec=pltpu.PrefetchScalarGridSpec(
            num_scalar_prefetch=1,
            grid=(features // tile,),
            in_specs=[column] * GROUP
            + [pl.BlockSpec(c.shape, lambda j, o: (0, 0, 0)) for c in columns]
            + [column, column],
            out_specs=[column] * len(kinds),
        ),
        out_shape=[jax.ShapeDtypeStruct((rows, features), kind) for kind in kinds],
        compiler_params=pltpu.CompilerParams(vmem_limit_bytes=48 * 2**20),
        name="refresh",
    )(order, *pieces, *columns, factor_old, row_old)


def place_kernel(order, *refs):
    count = order.shape[0]
    for k in range(count):
        @pl.when(pl.program_id(0) == k)
        def _():
            refs[-1][...] = refs[k][...]


def place_rows(order, pieces, base):
    rows, outputs = pieces[0].shape
    arrays = list(pieces) + ([] if base is None else [base])
    return pl.pallas_call(
        place_kernel,
        grid_spec=pltpu.PrefetchScalarGridSpec(
            num_scalar_prefetch=1,
            grid=(len(pieces),),
            in_specs=[pl.BlockSpec((rows, outputs), lambda j, o: (0, 0))] * len(pieces)
            + [pl.BlockSpec(memory_space=pl.ANY)] * (len(arrays) - len(pieces)),
            out_specs=pl.BlockSpec((rows, outputs), lambda j, o: (o[j], 0)),
        ),
        out_shape=jax.ShapeDtypeStruct((GROUP * rows, outputs), pieces[0].dtype),
        input_output_aliases={} if base is None else {len(arrays): 0},
        name="place_rows",
    )(order, *arrays)


def apply_kernel(order, *refs):
    pieces, matrices, (col_old, out, joined) = refs[:GROUP], refs[GROUP : GROUP + 3], refs[GROUP + 3 :]
    rows = pieces[0].shape[0]
    for k in range(GROUP):
        joined[pl.ds(pl.multiple_of(order[k] * rows, rows), rows), :] = pieces[k][...]
    full = joined[...]
    slim = rows // LAYERS
    diagonal = lax.broadcasted_iota(jnp.int32, (rows, rows), 0) == lax.broadcasted_iota(jnp.int32, (rows, rows), 1)
    old = None
    for k in range(GROUP):
        block = col_old[order[k]]
        block = jnp.where(diagonal, jnp.zeros_like(block), block) if k == 0 else block
        part = transposed_dot(block, pieces[k][...])
        old = part if k == 0 else old + part
    for n, matrix in enumerate(matrices):
        product = jnp.dot(matrix[...], full, preferred_element_type=F32)
        product = (product + FACTOR_DECAY * old if n == 1 else product).astype(BF16)
        for layer in range(LAYERS):
            out[layer, n * slim : (n + 1) * slim, :] = product[layer * slim : (layer + 1) * slim]


def apply_blocks(order, pieces, matrices, col_old):
    rows, outputs = pieces[0].shape
    features = matrices[0].shape[1]
    tile = 512
    slim = rows // LAYERS
    return pl.pallas_call(
        apply_kernel,
        grid_spec=pltpu.PrefetchScalarGridSpec(
            num_scalar_prefetch=1,
            grid=(outputs // tile,),
            in_specs=[pl.BlockSpec((rows, tile), lambda j, o: (0, j))] * GROUP
            + [pl.BlockSpec((rows, features), lambda j, o: (0, 0))] * 3
            + [pl.BlockSpec((GROUP, rows, rows), lambda j, o: (0, 0, 0))],
            out_specs=pl.BlockSpec((LAYERS, 3 * slim, tile), lambda j, o: (0, 0, j)),
            scratch_shapes=[pltpu.VMEM((features, tile), BF16)],
        ),
        out_shape=jax.ShapeDtypeStruct((LAYERS, 3 * slim, outputs), BF16),
        compiler_params=pltpu.CompilerParams(vmem_limit_bytes=48 * 2**20),
        name="apply_blocks",
    )(order, *pieces, *matrices, col_old)


def sweep(target, inverse, coupling, ratio, store):
    passed = jnp.zeros_like(target[0])
    scaled = []
    for layer in range(LAYERS):
        scaled.append((target[layer] - passed) * inverse[layer])
        passed = coupling[layer] * scaled[layer]
    nearer = jnp.zeros_like(passed)
    for layer in reversed(range(LAYERS)):
        nearer = scaled[layer] - ratio[layer] * nearer
        store(layer, nearer)


def initial_kernel(grad, pivots, inverse, coupling, ratio, solved):
    for start in range(0, grad.shape[-1], 128):
        lanes = pl.ds(start, 128)

        def store(layer, value):
            solved[layer, :, lanes] = value.astype(solved.dtype)

        sweep([grad[layer, :, lanes].astype(F32) for layer in range(LAYERS)], inverse, coupling, ratio, store)


def change_kernel(grad, initial, off, pivots, inverse, coupling, ratio, solved):
    slim = grad.shape[1]
    for start in range(0, grad.shape[-1], 128):
        lanes = pl.ds(start, 128)
        first = [initial[layer, :, lanes].astype(F32) for layer in range(LAYERS)]
        target = []
        for layer in range(LAYERS):
            applied = pivots[layer] * first[layer] + off[layer, :slim, lanes].astype(F32)
            if layer + 1 < LAYERS:
                applied = applied + coupling[layer] * first[layer + 1]
                applied = applied + off[layer + 1, 2 * slim : 3 * slim, lanes].astype(F32)
            if layer > 0:
                applied = applied + coupling[layer - 1] * first[layer - 1]
                applied = applied + off[layer - 1, slim : 2 * slim, lanes].astype(F32)
            target.append(grad[layer, :, lanes].astype(F32) - applied)

        def store(layer, value):
            solved[layer, :, lanes] = value.astype(solved.dtype)

        sweep(target, inverse, coupling, ratio, store)


def chain_solve(kernel, name, arrays, coefficients):
    return pl.pallas_call(
        kernel,
        out_shape=jax.ShapeDtypeStruct(arrays[0].shape, BF16),
        compiler_params=pltpu.CompilerParams(vmem_limit_bytes=32 * 2**20),
        name=name,
    )(*arrays, *coefficients)


def by_layer(value):
    return lax.all_to_all(value, LAYER, 0, 0)


def block_diagonal(block):
    return jnp.sum(jnp.where(jnp.eye(block.shape[0], dtype=bool), block, 0.0), axis=0)


def body(activations, factor_old, cross_old, gradients, moments, exponents, master):
    acts, factor_old, cross_old, grad = activations[0], factor_old[0], cross_old[0], gradients[0]
    rows, features = factor_old.shape
    outputs = grad.shape[1]
    slim = rows // LAYERS
    place = lax.axis_index(DP)
    start = place * rows
    weight = (1.0 - FACTOR_DECAY) / (rows * GROUP)
    order = piece_order()

    above = along_layers(acts, -1)
    before, beyond = turned(acts, 1), turned(acts, 3)
    grad_rows = by_layer(grad.reshape(LAYERS, slim, outputs))
    cross_blocks = cross_old.astype(BF16).reshape(rows, GROUP, rows).transpose(1, 0, 2)
    wide = acts.astype(F32)
    sums = jnp.stack([jnp.sum(wide * wide, axis=0), jnp.sum(wide * above.astype(F32), axis=0)])
    old_diagonals = jnp.stack(
        [block_diagonal(lax.dynamic_slice_in_dim(old, start, rows, 1)) for old in (factor_old, cross_old)]
    )
    here = (jnp.arange(GROUP) == place)[None, :, None]
    sums = weight * sums.reshape(2, GROUP, rows) + jnp.where(here, FACTOR_DECAY * old_diagonals[:, None, :], 0.0)
    message = sums.reshape(2, GROUP, LAYERS, slim).transpose(2, 1, 0, 3).reshape(LAYERS * GROUP, 2 * slim)
    message = jnp.pad(message, ((0, 0), (0, 128 - 2 * slim)))
    message, grad_rows, cross_blocks, shard = tied(message, grad_rows, cross_blocks, acts)
    other = across(shard)
    far = turned(before, 1)
    arrived = lax.all_to_all(message, LAYER + DP, 0, 0, tiled=True)
    arrived, other, far, before, beyond = tied(arrived, other, far, before, beyond)
    diagonals = jnp.sum(arrived.reshape(LAYERS, GROUP, 128), axis=1)[:, : 2 * slim].reshape(LAYERS, 2, slim)
    coupling = diagonals[:, 1]
    pivots = DAMPING + diagonals[:, 0]
    inverse = 1.0 / pivots
    coefficients = [
        jnp.broadcast_to(c[:, :, None], (LAYERS, slim, 128))
        for c in (pivots, inverse, coupling, coupling * inverse)
    ]

    initial_rows = chain_solve(initial_kernel, "first_solution", (grad_rows,), coefficients)
    initial_rows, other, far = tied(initial_rows, other, far)
    initial = by_layer(initial_rows).reshape(rows, outputs)

    remote = (far, turned(other, 1), turned(other, 3), across(far))
    initial, cross_slim, cross_blocks, *remote = tied(initial, cross_old.astype(BF16), cross_blocks, *remote)
    pieces = (shard, before, beyond, other, *remote)
    own = own_columns(order, pieces)
    columns = (own, along_layers(own, 1), along_layers(own, -1))
    row_old = along_layers(cross_slim, 1)
    col_old = lax.all_to_all(cross_blocks, DP, 0, 0, tiled=True)
    factor_new, factor_off, row_batch, row_off, col_off = refresh(
        weight, order, pieces, columns, factor_old, row_old
    )
    off = apply_blocks(order, gathered(initial), (factor_off, col_off, row_off), col_old)
    change_rows = chain_solve(change_kernel, "change", (grad_rows, initial_rows, by_layer(off)), coefficients)
    change_rows, row_batch = tied(change_rows, row_batch)
    change = by_layer(change_rows).reshape(rows, outputs)
    update = initial.astype(F32) + change.astype(F32)

    dequant = jnp.repeat(jnp.exp2(exponents[0].astype(F32)), SCALE_BLOCK)[:, None]
    requant = jnp.repeat(jnp.exp2(-exponents[0].astype(F32)), SCALE_BLOCK)[:, None]
    moment = MOMENTUM * moments[0].astype(F32) * dequant + (1.0 - MOMENTUM) * update
    moments_new = (moment * requant).astype(BF16)
    master_new = master[0] - STEP_SIZE * moment
    own = master_new.astype(BF16)
    other, before, beyond, far = tied(*first_round(own))
    cross_new = FACTOR_DECAY * cross_old + weight * along_layers(row_batch, -1).astype(F32)
    replicas = place_rows(order[:5], (own, before, beyond, other, far), None)
    replicas, cross_new = tied(replicas, cross_new)
    replicas = place_rows(order[5:], second_round(other, far), replicas)
    return (factor_new[None], cross_new[None], moments_new[None], master_new[None], replicas[None])


def solution(mesh):
    finer = Mesh(mesh.devices.reshape(2, 4, 2, 2, TURN), LAYER + DP)
    sharded = P(LAYER, DP, None)
    in_specs = (sharded,) * 5 + (P(LAYER, DP), sharded)
    out_specs = (sharded,) * 4 + (P(LAYER, None, None),)
    return jax.shard_map(body, mesh=finer, in_specs=in_specs, out_specs=out_specs, check_vma=False)
```

```python
import jax
import jax.numpy as jnp
from jax import lax
from jax.experimental import pallas as pl
from jax.experimental.pallas import tpu as pltpu
from jax.sharding import Mesh
from jax.sharding import PartitionSpec as P

SCALE_BLOCK = 128
LAYER = ("layer_0", "layer_1", "layer_2")
DP = ("dp_0", "dp_1")
LAYERS = 16
GROUP = 8
TURN = 4

FACTOR_DECAY = 0.9
DAMPING = 0.5
MOMENTUM = 0.8
STEP_SIZE = 0.05

F32 = jnp.float32
BF16 = jnp.bfloat16


def along_layers(value, steps):
    pairs = [(i, i + steps) for i in range(LAYERS) if 0 <= i + steps < LAYERS]
    return lax.ppermute(value, LAYER, pairs)


def turned(value, steps):
    return lax.ppermute(value, "dp_1", [(i, (i + steps) % TURN) for i in range(TURN)])


def across(value):
    return lax.ppermute(value, "dp_0", [(0, 1), (1, 0)])


def first_round(own):
    return across(own), turned(own, 1), turned(own, 3), turned(own, 2)


def second_round(other, far):
    return turned(other, 1), turned(other, 3), across(far)


def gathered(own):
    other, before, beyond, far = tied(*first_round(own))
    return own, before, beyond, other, far, *second_round(other, far)


def piece_order():
    mine, turn = lax.axis_index("dp_0"), lax.axis_index("dp_1")
    side = jnp.stack([mine] * 3 + [1 - mine, mine] + [1 - mine] * 3)
    steps = jnp.array([0, 3, 1, 0, 2, 3, 1, 2], jnp.int32)
    return (side * TURN + (turn + steps) % TURN).astype(jnp.int32)


def tied(*values):
    return lax.optimization_barrier(values)


def transposed_dot(left, right):
    return lax.dot_general(left, right, (((0,), (0,)), ((), ())), preferred_element_type=F32)


def pick_kernel(order, *refs):
    for k, piece in enumerate(refs[:-1]):
        refs[-1][k] = piece[...]


def own_columns(order, pieces):
    rows = pieces[0].shape[0]
    return pl.pallas_call(
        pick_kernel,
        grid_spec=pltpu.PrefetchScalarGridSpec(
            num_scalar_prefetch=1,
            grid=(1,),
            in_specs=[pl.BlockSpec((rows, rows), lambda j, o: (0, o[0]))] * len(pieces),
            out_specs=pl.BlockSpec((len(pieces), rows, rows), lambda j, o: (0, 0, 0)),
        ),
        out_shape=jax.ShapeDtypeStruct((len(pieces), rows, rows), pieces[0].dtype),
        name="own_columns",
    )(order, *pieces)


def refresh_kernel(weight, order, *refs):
    pieces, columns, (factor_old, row_old) = refs[:GROUP], refs[GROUP : GROUP + 3], refs[GROUP + 3 : GROUP + 5]
    factor, factor_off, row_batch, row_off, col_off = refs[GROUP + 5 :]
    sums = [None, None, None]
    for k in range(GROUP):
        right = pieces[k][...]
        for n in range(3):
            part = transposed_dot(columns[n][k], right)
            sums[n] = part if k == 0 else sums[n] + part
    rows, tile = factor.shape
    column = pl.program_id(0) * tile + lax.broadcasted_iota(jnp.int32, (rows, tile), 1)
    diagonal = column == order[0] * rows + lax.broadcasted_iota(jnp.int32, (rows, tile), 0)
    fresh = FACTOR_DECAY * factor_old[...] + weight * sums[0]
    factor[...] = fresh
    factor_off[...] = jnp.where(diagonal, 0.0, fresh).astype(BF16)
    row_batch[...] = sums[1].astype(BF16)
    row = FACTOR_DECAY * row_old[...].astype(F32) + weight * sums[1]
    row_off[...] = jnp.where(diagonal, 0.0, row).astype(BF16)
    col_off[...] = jnp.where(diagonal, 0.0, weight * sums[2]).astype(BF16)


def refresh(weight, order, pieces, columns, factor_old, row_old):
    rows, features = factor_old.shape
    tile = 512
    column = pl.BlockSpec((rows, tile), lambda j, o: (0, j))
    kinds = (F32, BF16, BF16, BF16, BF16)
    return pl.pallas_call(
        lambda *refs: refresh_kernel(weight, *refs),
        grid_spec=pltpu.PrefetchScalarGridSpec(
            num_scalar_prefetch=1,
            grid=(features // tile,),
            in_specs=[column] * GROUP
            + [pl.BlockSpec(c.shape, lambda j, o: (0, 0, 0)) for c in columns]
            + [column, column],
            out_specs=[column] * len(kinds),
        ),
        out_shape=[jax.ShapeDtypeStruct((rows, features), kind) for kind in kinds],
        compiler_params=pltpu.CompilerParams(vmem_limit_bytes=60 * 2**20),
        name="refresh",
    )(order, *pieces, *columns, factor_old, row_old)


def place_kernel(order, *refs):
    count = order.shape[0]
    for k in range(count):
        @pl.when(pl.program_id(0) == k)
        def _():
            refs[-1][...] = refs[k][...]


def place_rows(order, pieces, base):
    rows, outputs = pieces[0].shape
    arrays = list(pieces) + ([] if base is None else [base])
    return pl.pallas_call(
        place_kernel,
        grid_spec=pltpu.PrefetchScalarGridSpec(
            num_scalar_prefetch=1,
            grid=(len(pieces),),
            in_specs=[pl.BlockSpec((rows, outputs), lambda j, o: (0, 0))] * len(pieces)
            + [pl.BlockSpec(memory_space=pl.ANY)] * (len(arrays) - len(pieces)),
            out_specs=pl.BlockSpec((rows, outputs), lambda j, o: (o[j], 0)),
        ),
        out_shape=jax.ShapeDtypeStruct((GROUP * rows, outputs), pieces[0].dtype),
        input_output_aliases={} if base is None else {len(arrays): 0},
        name="place_rows",
    )(order, *arrays)


def apply_kernel(order, *refs):
    pieces, matrices, (col_old, out, joined) = refs[:GROUP], refs[GROUP : GROUP + 3], refs[GROUP + 3 :]
    rows = pieces[0].shape[0]
    for k in range(GROUP):
        joined[pl.ds(pl.multiple_of(order[k] * rows, rows), rows), :] = pieces[k][...]
    full = joined[...]
    slim = rows // LAYERS
    diagonal = lax.broadcasted_iota(jnp.int32, (rows, rows), 0) == lax.broadcasted_iota(jnp.int32, (rows, rows), 1)
    old = None
    for k in range(GROUP):
        block = col_old[order[k]]
        block = jnp.where(diagonal, jnp.zeros_like(block), block) if k == 0 else block
        part = transposed_dot(block, pieces[k][...])
        old = part if k == 0 else old + part
    for n, matrix in enumerate(matrices):
        product = jnp.dot(matrix[...], full, preferred_element_type=F32)
        product = (product + FACTOR_DECAY * old if n == 1 else product).astype(BF16)
        for layer in range(LAYERS):
            out[layer, n * slim : (n + 1) * slim, :] = product[layer * slim : (layer + 1) * slim]


def apply_blocks(order, pieces, matrices, col_old):
    rows, outputs = pieces[0].shape
    features = matrices[0].shape[1]
    tile = 512
    slim = rows // LAYERS
    return pl.pallas_call(
        apply_kernel,
        grid_spec=pltpu.PrefetchScalarGridSpec(
            num_scalar_prefetch=1,
            grid=(outputs // tile,),
            in_specs=[pl.BlockSpec((rows, tile), lambda j, o: (0, j))] * GROUP
            + [pl.BlockSpec((rows, features), lambda j, o: (0, 0))] * 3
            + [pl.BlockSpec((GROUP, rows, rows), lambda j, o: (0, 0, 0))],
            out_specs=pl.BlockSpec((LAYERS, 3 * slim, tile), lambda j, o: (0, 0, j)),
            scratch_shapes=[pltpu.VMEM((features, tile), BF16)],
        ),
        out_shape=jax.ShapeDtypeStruct((LAYERS, 3 * slim, outputs), BF16),
        compiler_params=pltpu.CompilerParams(vmem_limit_bytes=60 * 2**20),
        name="apply_blocks",
    )(order, *pieces, *matrices, col_old)


def sweep(target, inverse, coupling, ratio, store):
    passed = jnp.zeros_like(target[0])
    scaled = []
    for layer in range(LAYERS):
        scaled.append((target[layer] - passed) * inverse[layer])
        passed = coupling[layer] * scaled[layer]
    nearer = jnp.zeros_like(passed)
    for layer in reversed(range(LAYERS)):
        nearer = scaled[layer] - ratio[layer] * nearer
        store(layer, nearer)


def initial_kernel(grad, pivots, inverse, coupling, ratio, solved):
    for start in range(0, grad.shape[-1], 128):
        lanes = pl.ds(start, 128)

        def store(layer, value):
            solved[layer, :, lanes] = value.astype(solved.dtype)

        sweep([grad[layer, :, lanes].astype(F32) for layer in range(LAYERS)], inverse, coupling, ratio, store)


def change_kernel(grad, initial, off, pivots, inverse, coupling, ratio, solved):
    slim = grad.shape[1]
    for start in range(0, grad.shape[-1], 128):
        lanes = pl.ds(start, 128)
        first = [initial[layer, :, lanes].astype(F32) for layer in range(LAYERS)]
        target = []
        for layer in range(LAYERS):
            applied = pivots[layer] * first[layer] + off[layer, :slim, lanes].astype(F32)
            if layer + 1 < LAYERS:
                applied = applied + coupling[layer] * first[layer + 1]
                applied = applied + off[layer + 1, 2 * slim : 3 * slim, lanes].astype(F32)
            if layer > 0:
                applied = applied + coupling[layer - 1] * first[layer - 1]
                applied = applied + off[layer - 1, slim : 2 * slim, lanes].astype(F32)
            target.append(grad[layer, :, lanes].astype(F32) - applied)

        def store(layer, value):
            solved[layer, :, lanes] = value.astype(solved.dtype)

        sweep(target, inverse, coupling, ratio, store)


def chain_solve(kernel, name, arrays, coefficients):
    return pl.pallas_call(
        kernel,
        out_shape=jax.ShapeDtypeStruct(arrays[0].shape, BF16),
        compiler_params=pltpu.CompilerParams(vmem_limit_bytes=32 * 2**20),
        name=name,
    )(*arrays, *coefficients)


def by_layer(value):
    return lax.all_to_all(value, LAYER, 0, 0)


def block_diagonal(block):
    return jnp.sum(jnp.where(jnp.eye(block.shape[0], dtype=bool), block, 0.0), axis=0)


def body(activations, factor_old, cross_old, gradients, moments, exponents, master):
    acts, factor_old, cross_old, grad = activations[0], factor_old[0], cross_old[0], gradients[0]
    rows, features = factor_old.shape
    outputs = grad.shape[1]
    slim = rows // LAYERS
    place = lax.axis_index(DP)
    start = place * rows
    weight = (1.0 - FACTOR_DECAY) / (rows * GROUP)
    order = piece_order()

    above = along_layers(acts, -1)
    before, beyond = turned(acts, 1), turned(acts, 3)
    grad_rows = by_layer(grad.reshape(LAYERS, slim, outputs))
    cross_blocks = cross_old.astype(BF16).reshape(rows, GROUP, rows).transpose(1, 0, 2)
    wide = acts.astype(F32)
    sums = jnp.stack([jnp.sum(wide * wide, axis=0), jnp.sum(wide * above.astype(F32), axis=0)])
    old_diagonals = jnp.stack(
        [block_diagonal(lax.dynamic_slice_in_dim(old, start, rows, 1)) for old in (factor_old, cross_old)]
    )
    here = (jnp.arange(GROUP) == place)[None, :, None]
    sums = weight * sums.reshape(2, GROUP, rows) + jnp.where(here, FACTOR_DECAY * old_diagonals[:, None, :], 0.0)
    message = sums.reshape(2, GROUP, LAYERS, slim).transpose(2, 1, 0, 3).reshape(LAYERS * GROUP, 2 * slim)
    message = jnp.pad(message, ((0, 0), (0, 128 - 2 * slim)))
    message, grad_rows, cross_blocks, shard = tied(message, grad_rows, cross_blocks, acts)
    other = across(shard)
    far = turned(before, 1)
    arrived = lax.all_to_all(message, LAYER + DP, 0, 0, tiled=True)
    arrived, other, far, before, beyond = tied(arrived, other, far, before, beyond)
    diagonals = jnp.sum(arrived.reshape(LAYERS, GROUP, 128), axis=1)[:, : 2 * slim].reshape(LAYERS, 2, slim)
    coupling = diagonals[:, 1]
    pivots = DAMPING + diagonals[:, 0]
    inverse = 1.0 / pivots
    coefficients = [
        jnp.broadcast_to(c[:, :, None], (LAYERS, slim, 128))
        for c in (pivots, inverse, coupling, coupling * inverse)
    ]

    initial_rows = chain_solve(initial_kernel, "first_solution", (grad_rows,), coefficients)
    initial_rows, other, far = tied(initial_rows, other, far)
    initial = by_layer(initial_rows).reshape(rows, outputs)

    remote = (far, turned(other, 1), turned(other, 3), across(far))
    initial, cross_slim, cross_blocks, *remote = tied(initial, cross_old.astype(BF16), cross_blocks, *remote)
    pieces = (shard, before, beyond, other, *remote)
    own = own_columns(order, pieces)
    columns = (own, along_layers(own, 1), along_layers(own, -1))
    row_old = along_layers(cross_slim, 1)
    col_old = lax.all_to_all(cross_blocks, DP, 0, 0, tiled=True)
    factor_new, factor_off, row_batch, row_off, col_off = refresh(
        weight, order, pieces, columns, factor_old, row_old
    )
    off = apply_blocks(order, gathered(initial), (factor_off, col_off, row_off), col_old)
    change_rows = chain_solve(change_kernel, "change", (grad_rows, initial_rows, by_layer(off)), coefficients)
    change_rows, row_batch = tied(change_rows, row_batch)
    change = by_layer(change_rows).reshape(rows, outputs)
    update = initial.astype(F32) + change.astype(F32)

    dequant = jnp.repeat(jnp.exp2(exponents[0].astype(F32)), SCALE_BLOCK)[:, None]
    requant = jnp.repeat(jnp.exp2(-exponents[0].astype(F32)), SCALE_BLOCK)[:, None]
    moment = MOMENTUM * moments[0].astype(F32) * dequant + (1.0 - MOMENTUM) * update
    moments_new = (moment * requant).astype(BF16)
    master_new = master[0] - STEP_SIZE * moment
    own = master_new.astype(BF16)
    other, before, beyond, far = tied(*first_round(own))
    cross_new = FACTOR_DECAY * cross_old + weight * along_layers(row_batch, -1).astype(F32)
    replicas = place_rows(order[:5], (own, before, beyond, other, far), None)
    replicas, cross_new = tied(replicas, cross_new)
    replicas = place_rows(order[5:], second_round(other, far), replicas)
    return (factor_new[None], cross_new[None], moments_new[None], master_new[None], replicas[None])


def solution(mesh):
    finer = Mesh(mesh.devices.reshape(2, 4, 2, 2, TURN), LAYER + DP)
    sharded = P(LAYER, DP, None)
    in_specs = (sharded,) * 5 + (P(LAYER, DP), sharded)
    out_specs = (sharded,) * 4 + (P(LAYER, None, None),)
    return jax.shard_map(body, mesh=finer, in_specs=in_specs, out_specs=out_specs, check_vma=False)
```

```python
import jax
import jax.numpy as jnp
from jax import lax
from jax.experimental import pallas as pl
from jax.experimental.pallas import tpu as pltpu
from jax.sharding import Mesh
from jax.sharding import PartitionSpec as P

SCALE_BLOCK = 128
LAYER = ("layer_0", "layer_1", "layer_2")
DP = ("dp_0", "dp_1")
LAYERS = 16
GROUP = 8
TURN = 4

FACTOR_DECAY = 0.9
DAMPING = 0.5
MOMENTUM = 0.8
STEP_SIZE = 0.05

F32 = jnp.float32
BF16 = jnp.bfloat16


def along_layers(value, steps):
    pairs = [(i, i + steps) for i in range(LAYERS) if 0 <= i + steps < LAYERS]
    return lax.ppermute(value, LAYER, pairs)


def turned(value, steps):
    return lax.ppermute(value, "dp_1", [(i, (i + steps) % TURN) for i in range(TURN)])


def across(value):
    return lax.ppermute(value, "dp_0", [(0, 1), (1, 0)])


def first_round(own):
    return across(own), turned(own, 1), turned(own, 3), turned(own, 2)


def second_round(other, far):
    return turned(other, 1), turned(other, 3), across(far)


def gathered(own):
    other, before, beyond, far = tied(*first_round(own))
    return own, before, beyond, other, far, *second_round(other, far)


def piece_order():
    mine, turn = lax.axis_index("dp_0"), lax.axis_index("dp_1")
    side = jnp.stack([mine] * 3 + [1 - mine, mine] + [1 - mine] * 3)
    steps = jnp.array([0, 3, 1, 0, 2, 3, 1, 2], jnp.int32)
    return (side * TURN + (turn + steps) % TURN).astype(jnp.int32)


def tied(*values):
    return lax.optimization_barrier(values)


def transposed_dot(left, right):
    return lax.dot_general(left, right, (((0,), (0,)), ((), ())), preferred_element_type=F32)


def pick_kernel(order, *refs):
    for k, piece in enumerate(refs[:-1]):
        refs[-1][k] = piece[...]


def own_columns(order, pieces):
    rows = pieces[0].shape[0]
    return pl.pallas_call(
        pick_kernel,
        grid_spec=pltpu.PrefetchScalarGridSpec(
            num_scalar_prefetch=1,
            grid=(1,),
            in_specs=[pl.BlockSpec((rows, rows), lambda j, o: (0, o[0]))] * len(pieces),
            out_specs=pl.BlockSpec((len(pieces), rows, rows), lambda j, o: (0, 0, 0)),
        ),
        out_shape=jax.ShapeDtypeStruct((len(pieces), rows, rows), pieces[0].dtype),
        name="own_columns",
    )(order, *pieces)


def refresh_kernel(weight, order, *refs):
    pieces, columns, (factor_old, row_old) = refs[:GROUP], refs[GROUP : GROUP + 3], refs[GROUP + 3 : GROUP + 5]
    factor, factor_off, row_batch, row_off, col_off = refs[GROUP + 5 :]
    sums = [None, None, None]
    for k in range(GROUP):
        right = pieces[k][...]
        for n in range(3):
            part = transposed_dot(columns[n][k], right)
            sums[n] = part if k == 0 else sums[n] + part
    rows, tile = factor.shape
    column = pl.program_id(0) * tile + lax.broadcasted_iota(jnp.int32, (rows, tile), 1)
    diagonal = column == order[0] * rows + lax.broadcasted_iota(jnp.int32, (rows, tile), 0)
    fresh = FACTOR_DECAY * factor_old[...] + weight * sums[0]
    factor[...] = fresh
    factor_off[...] = jnp.where(diagonal, 0.0, fresh).astype(BF16)
    row_batch[...] = sums[1].astype(BF16)
    row = FACTOR_DECAY * row_old[...].astype(F32) + weight * sums[1]
    row_off[...] = jnp.where(diagonal, 0.0, row).astype(BF16)
    col_off[...] = jnp.where(diagonal, 0.0, weight * sums[2]).astype(BF16)


def refresh(weight, order, pieces, columns, factor_old, row_old):
    rows, features = factor_old.shape
    tile = 512
    column = pl.BlockSpec((rows, tile), lambda j, o: (0, j))
    kinds = (F32, BF16, BF16, BF16, BF16)
    return pl.pallas_call(
        lambda *refs: refresh_kernel(weight, *refs),
        grid_spec=pltpu.PrefetchScalarGridSpec(
            num_scalar_prefetch=1,
            grid=(features // tile,),
            in_specs=[column] * GROUP
            + [pl.BlockSpec(c.shape, lambda j, o: (0, 0, 0)) for c in columns]
            + [column, column],
            out_specs=[column] * len(kinds),
        ),
        out_shape=[jax.ShapeDtypeStruct((rows, features), kind) for kind in kinds],
        compiler_params=pltpu.CompilerParams(vmem_limit_bytes=60 * 2**20),
        name="refresh",
    )(order, *pieces, *columns, factor_old, row_old)


def place_kernel(order, *refs):
    count = order.shape[0]
    for k in range(count):
        @pl.when(pl.program_id(0) == k)
        def _():
            refs[-1][...] = refs[k][...]


def place_rows(order, pieces, base):
    rows, outputs = pieces[0].shape
    arrays = list(pieces) + ([] if base is None else [base])
    return pl.pallas_call(
        place_kernel,
        grid_spec=pltpu.PrefetchScalarGridSpec(
            num_scalar_prefetch=1,
            grid=(len(pieces),),
            in_specs=[pl.BlockSpec((rows, outputs), lambda j, o: (0, 0))] * len(pieces)
            + [pl.BlockSpec(memory_space=pl.ANY)] * (len(arrays) - len(pieces)),
            out_specs=pl.BlockSpec((rows, outputs), lambda j, o: (o[j], 0)),
        ),
        out_shape=jax.ShapeDtypeStruct((GROUP * rows, outputs), pieces[0].dtype),
        input_output_aliases={} if base is None else {len(arrays): 0},
        name="place_rows",
    )(order, *arrays)


def apply_kernel(order, *refs):
    pieces, matrices, (col_old, out, joined) = refs[:GROUP], refs[GROUP : GROUP + 3], refs[GROUP + 3 :]
    rows = pieces[0].shape[0]
    for k in range(GROUP):
        joined[pl.ds(pl.multiple_of(order[k] * rows, rows), rows), :] = pieces[k][...]
    full = joined[...]
    slim = rows // LAYERS
    diagonal = lax.broadcasted_iota(jnp.int32, (rows, rows), 0) == lax.broadcasted_iota(jnp.int32, (rows, rows), 1)
    old = None
    for k in range(GROUP):
        block = col_old[order[k]]
        block = jnp.where(diagonal, jnp.zeros_like(block), block) if k == 0 else block
        part = transposed_dot(block, pieces[k][...])
        old = part if k == 0 else old + part
    for n, matrix in enumerate(matrices):
        product = jnp.dot(matrix[...], full, preferred_element_type=F32)
        product = (product + FACTOR_DECAY * old if n == 1 else product).astype(BF16)
        for layer in range(LAYERS):
            out[layer, n * slim : (n + 1) * slim, :] = product[layer * slim : (layer + 1) * slim]


def apply_blocks(order, pieces, matrices, col_old):
    rows, outputs = pieces[0].shape
    features = matrices[0].shape[1]
    tile = 512
    slim = rows // LAYERS
    return pl.pallas_call(
        apply_kernel,
        grid_spec=pltpu.PrefetchScalarGridSpec(
            num_scalar_prefetch=1,
            grid=(outputs // tile,),
            in_specs=[pl.BlockSpec((rows, tile), lambda j, o: (0, j))] * GROUP
            + [pl.BlockSpec((rows, features), lambda j, o: (0, 0))] * 3
            + [pl.BlockSpec((GROUP, rows, rows), lambda j, o: (0, 0, 0))],
            out_specs=pl.BlockSpec((LAYERS, 3 * slim, tile), lambda j, o: (0, 0, j)),
            scratch_shapes=[pltpu.VMEM((features, tile), BF16)],
        ),
        out_shape=jax.ShapeDtypeStruct((LAYERS, 3 * slim, outputs), BF16),
        compiler_params=pltpu.CompilerParams(vmem_limit_bytes=60 * 2**20),
        name="apply_blocks",
    )(order, *pieces, *matrices, col_old)


def sweep(target, inverse, coupling, ratio, store):
    passed = jnp.zeros_like(target[0])
    scaled = []
    for layer in range(LAYERS):
        scaled.append((target[layer] - passed) * inverse[layer])
        passed = coupling[layer] * scaled[layer]
    nearer = jnp.zeros_like(passed)
    for layer in reversed(range(LAYERS)):
        nearer = scaled[layer] - ratio[layer] * nearer
        store(layer, nearer)


def initial_kernel(grad, pivots, inverse, coupling, ratio, solved):
    for start in range(0, grad.shape[-1], 128):
        lanes = pl.ds(start, 128)

        def store(layer, value):
            solved[layer, :, lanes] = value.astype(solved.dtype)

        sweep([grad[layer, :, lanes].astype(F32) for layer in range(LAYERS)], inverse, coupling, ratio, store)


def change_kernel(grad, initial, off, pivots, inverse, coupling, ratio, solved):
    slim = grad.shape[1]
    for start in range(0, grad.shape[-1], 128):
        lanes = pl.ds(start, 128)
        first = [initial[layer, :, lanes].astype(F32) for layer in range(LAYERS)]
        target = []
        for layer in range(LAYERS):
            applied = pivots[layer] * first[layer] + off[layer, :slim, lanes].astype(F32)
            if layer + 1 < LAYERS:
                applied = applied + coupling[layer] * first[layer + 1]
                applied = applied + off[layer + 1, 2 * slim : 3 * slim, lanes].astype(F32)
            if layer > 0:
                applied = applied + coupling[layer - 1] * first[layer - 1]
                applied = applied + off[layer - 1, slim : 2 * slim, lanes].astype(F32)
            target.append(grad[layer, :, lanes].astype(F32) - applied)

        def store(layer, value):
            solved[layer, :, lanes] = value.astype(solved.dtype)

        sweep(target, inverse, coupling, ratio, store)


def chain_solve(kernel, name, arrays, coefficients):
    return pl.pallas_call(
        kernel,
        out_shape=jax.ShapeDtypeStruct(arrays[0].shape, BF16),
        compiler_params=pltpu.CompilerParams(vmem_limit_bytes=60 * 2**20),
        name=name,
    )(*arrays, *coefficients)


def by_layer(value):
    return lax.all_to_all(value, LAYER, 0, 0)


def block_diagonal(block):
    return jnp.sum(jnp.where(jnp.eye(block.shape[0], dtype=bool), block, 0.0), axis=0)


def body(activations, factor_old, cross_old, gradients, moments, exponents, master):
    acts, factor_old, cross_old, grad = activations[0], factor_old[0], cross_old[0], gradients[0]
    rows, features = factor_old.shape
    outputs = grad.shape[1]
    slim = rows // LAYERS
    place = lax.axis_index(DP)
    start = place * rows
    weight = (1.0 - FACTOR_DECAY) / (rows * GROUP)
    order = piece_order()

    above = along_layers(acts, -1)
    before, beyond = turned(acts, 1), turned(acts, 3)
    grad_rows = by_layer(grad.reshape(LAYERS, slim, outputs))
    cross_blocks = cross_old.astype(BF16).reshape(rows, GROUP, rows).transpose(1, 0, 2)
    wide = acts.astype(F32)
    sums = jnp.stack([jnp.sum(wide * wide, axis=0), jnp.sum(wide * above.astype(F32), axis=0)])
    old_diagonals = jnp.stack(
        [block_diagonal(lax.dynamic_slice_in_dim(old, start, rows, 1)) for old in (factor_old, cross_old)]
    )
    here = (jnp.arange(GROUP) == place)[None, :, None]
    sums = weight * sums.reshape(2, GROUP, rows) + jnp.where(here, FACTOR_DECAY * old_diagonals[:, None, :], 0.0)
    message = sums.reshape(2, GROUP, LAYERS, slim).transpose(2, 1, 0, 3).reshape(LAYERS * GROUP, 2 * slim)
    message = jnp.pad(message, ((0, 0), (0, 128 - 2 * slim)))
    message, grad_rows, cross_blocks, shard = tied(message, grad_rows, cross_blocks, acts)
    other = across(shard)
    far = turned(before, 1)
    arrived = lax.all_to_all(message, LAYER + DP, 0, 0, tiled=True)
    arrived, other, far, before, beyond = tied(arrived, other, far, before, beyond)
    diagonals = jnp.sum(arrived.reshape(LAYERS, GROUP, 128), axis=1)[:, : 2 * slim].reshape(LAYERS, 2, slim)
    coupling = diagonals[:, 1]
    pivots = DAMPING + diagonals[:, 0]
    inverse = 1.0 / pivots
    coefficients = [
        jnp.broadcast_to(c[:, :, None], (LAYERS, slim, 128))
        for c in (pivots, inverse, coupling, coupling * inverse)
    ]

    initial_rows = chain_solve(initial_kernel, "first_solution", (grad_rows,), coefficients)
    initial_rows, other, far = tied(initial_rows, other, far)
    initial = by_layer(initial_rows).reshape(rows, outputs)

    remote = (far, turned(other, 1), turned(other, 3), across(far))
    initial, cross_slim, cross_blocks, *remote = tied(initial, cross_old.astype(BF16), cross_blocks, *remote)
    pieces = (shard, before, beyond, other, *remote)
    own = own_columns(order, pieces)
    columns = (own, along_layers(own, 1), along_layers(own, -1))
    row_old = along_layers(cross_slim, 1)
    col_old = lax.all_to_all(cross_blocks, DP, 0, 0, tiled=True)
    factor_new, factor_off, row_batch, row_off, col_off = refresh(
        weight, order, pieces, columns, factor_old, row_old
    )
    off = apply_blocks(order, gathered(initial), (factor_off, col_off, row_off), col_old)
    change_rows = chain_solve(change_kernel, "change", (grad_rows, initial_rows, by_layer(off)), coefficients)
    change_rows, row_batch = tied(change_rows, row_batch)
    change = by_layer(change_rows).reshape(rows, outputs)
    update = initial.astype(F32) + change.astype(F32)

    dequant = jnp.repeat(jnp.exp2(exponents[0].astype(F32)), SCALE_BLOCK)[:, None]
    requant = jnp.repeat(jnp.exp2(-exponents[0].astype(F32)), SCALE_BLOCK)[:, None]
    moment = MOMENTUM * moments[0].astype(F32) * dequant + (1.0 - MOMENTUM) * update
    moments_new = (moment * requant).astype(BF16)
    master_new = master[0] - STEP_SIZE * moment
    own = master_new.astype(BF16)
    other, before, beyond, far = tied(*first_round(own))
    cross_new = FACTOR_DECAY * cross_old + weight * along_layers(row_batch, -1).astype(F32)
    replicas = place_rows(order[:5], (own, before, beyond, other, far), None)
    replicas, cross_new = tied(replicas, cross_new)
    replicas = place_rows(order[5:], second_round(other, far), replicas)
    return (factor_new[None], cross_new[None], moments_new[None], master_new[None], replicas[None])


def solution(mesh):
    finer = Mesh(mesh.devices.reshape(2, 4, 2, 2, TURN), LAYER + DP)
    sharded = P(LAYER, DP, None)
    in_specs = (sharded,) * 5 + (P(LAYER, DP), sharded)
    out_specs = (sharded,) * 4 + (P(LAYER, None, None),)
    return jax.shard_map(body, mesh=finer, in_specs=in_specs, out_specs=out_specs, check_vma=False)
```
